128 devices in a mesh: space: 8 (over x, core), tile: 16 (over y, z).
Axes of the slice: x: 4, y: 4, z: 4, core: 2. Of those that a mesh axis runs over, the one named last changes fastest.
Arguments:
- atom_feat: bfloat16 [2048, 128, 128], P(('space', 'tile')), may hold values from -6 to 6
- atom_pos: bfloat16 [2048, 3, 128], P(('space', 'tile')), may hold values from 0 to 4
- atom_counts: int32 [2048], P(('space', 'tile')), may hold values from 32 to 128
- atom_nbrs: int32 [2048, 4], P(('space', 'tile')), may hold values from 0 to 2047, as said below
- probe_pos: float32 [256, 3, 512], P(('space', 'tile')), may hold values from 0 to 4
- probe_target: float32 [256, 512], P(('space', 'tile')), may hold values from -6 to 6
- tile_blocks: int32 [256, 8], P(('space', 'tile')), may hold values from 0 to 2047, as said below
- atom_filter: bfloat16 [128, 1024], replicated, may hold values from -0.5 to 0.5
- probe_filter: bfloat16 [128, 1024], replicated, may hold values from -0.5 to 0.5
- mix_weight: bfloat16 [128, 128], replicated, may hold values from -0.5 to 0.5
- readout: float32 [128], replicated, may hold values from -0.5 to 0.5
Outputs:
- density: float32 [256, 512], P(('space', 'tile'))
- atom_filter_grad: float32 [128, 1024], replicated
- probe_filter_grad: float32 [128, 1024], replicated
- mix_grad: float32 [128, 128], replicated
- readout_grad: float32 [128], replicated
The draws below stay inside these ranges and needn't reach their ends.
Inputs may be any that keep to these rules, and one draw needn't show every extreme that they name: `atom_nbrs`: block g lies on device g // 16 in the order space then tile. The 4 neighbours of a block lie on devices of the same tile index whose space index differs by at most one, cyclically: the first one lower, the second one higher, the third the same; they need not be distinct. `tile_blocks`: the 8 blocks of a tile are distinct and lie on devices of the tile's own space index. The tiles of one device read at most 2 distinct blocks from any one device, and exactly 2 from some device.
All inputs are finite; a program needn't handle non-finite values.
Results may differ from the reference program's by a relative error of at most 0.0061.
Values may be sent and summed in bfloat16 or wider, within the bound.
No kernel may reach another device: no remote copies, remote signals or barrier semaphores. Data moves between devices by JAX's collectives and lax.ppermute only.
A program may use at most 64 MiB of HBM per device.

```python
import jax
import jax.numpy as jnp
from jax import lax

C = 128
NRAD = 8
ABLK = 128
PT = 512
KB = 8
KA = 4
BLK_DEV = 16
TL_DEV = 2
RCAP = 2
BLOCKS = 2048
TILES = 256
N_SPACE = 8
N_TILE = 16
DEVICES = 128


def draw_atom_nbrs(key, part):
    block_ids = jnp.arange(BLOCKS)
    space_of = block_ids // (N_TILE * BLK_DEV)
    tile_of = block_ids // BLK_DEV % N_TILE
    first_key, second_key = jax.random.split(jax.random.fold_in(key, 11))
    extra = jax.random.randint(first_key, (BLOCKS, KA - 3), -1, 2).astype(jnp.int32)
    shifts = jnp.concatenate([jnp.full((BLOCKS, 1), -1, jnp.int32), jnp.full((BLOCKS, 1), 1, jnp.int32), jnp.zeros((BLOCKS, 1), jnp.int32), extra], axis=1)
    within = jax.random.randint(second_key, (BLOCKS, KA), 0, BLK_DEV).astype(jnp.int32)
    target_space = (space_of[:, None] + shifts + N_SPACE) % N_SPACE
    return ((target_space * N_TILE + tile_of[:, None]) * BLK_DEV + within).astype(jnp.int32)


def draw_tile_blocks(key, part):
    slot_count = TL_DEV * KB
    unit_count = N_TILE * RCAP

    def one_device(device_key, device):
        split_keys = jax.random.split(device_key, 4)
        unit_peer = jnp.arange(unit_count) // RCAP
        favoured = jax.random.randint(split_keys[0], (), 0, N_TILE)
        priority = jax.random.randint(split_keys[1], (unit_count,), 0, 2 ** 20) * unit_count + jnp.arange(unit_count)
        priority = jnp.where(unit_peer == favoured, jnp.arange(unit_count) - unit_count, priority)
        picked = jnp.argsort(priority, stable=True)[:slot_count]
        peer_ids = unit_peer[picked]
        earlier = jnp.tril(jnp.ones((slot_count, slot_count), jnp.int32), -1)
        peer_rank = jnp.sum(earlier * (peer_ids[:, None] == peer_ids[None, :]).astype(jnp.int32), axis=1)
        orders = jax.vmap(lambda peer_key: jax.random.permutation(peer_key, BLK_DEV))(jax.random.split(split_keys[2], N_TILE))
        within = orders[peer_ids, peer_rank]
        region = device // N_TILE
        blocks = (region * N_TILE + peer_ids) * BLK_DEV + within
        shuffled = blocks[jax.random.permutation(split_keys[3], slot_count)]
        return shuffled.reshape(TL_DEV, KB)
    device_keys = jax.random.split(jax.random.fold_in(key, 23), DEVICES)
    return jax.vmap(one_device)(device_keys, jnp.arange(DEVICES)).reshape(TILES, KB).astype(jnp.int32)


def plant(entries, own_key, low, largest):
    shape = entries.shape
    spot = [jax.random.randint(jax.random.fold_in(own_key, axis), (), 0, shape[axis]) for axis in range(len(shape))]
    entries = entries.at[tuple(spot)].set(low)
    longest = shape.index(max(shape))
    spot[longest] = (spot[longest] + 1) % shape[longest]
    return entries.at[tuple(spot)].set(largest)


def level_of(own_key, extent, cuts, least, top_value):
    def one(dim, parts):
        steps = jax.random.uniform(jax.random.fold_in(jax.random.fold_in(own_key, 6), dim), (parts,), jnp.float32, least / len(cuts), top_value / len(cuts))
        return jnp.repeat(jnp.exp(steps), extent[dim] // parts).reshape((-1,) + (1,) * (len(extent) - dim - 1))

    level = one(*cuts[0])
    for cut in cuts[1:]:
        level = level * one(*cut)
    return level


def normal_values(stream_key, dims, deviation, reach, cuts=(), kind=jnp.bfloat16):
    entries = jax.random.normal(stream_key, dims, jnp.float32) * deviation
    if len(cuts) > 0:
        entries = level_of(stream_key, dims, cuts, -0.22, 0.18) * entries
    return jnp.clip(entries, min=-reach, max=reach).astype(kind)


def setup_inputs(seed: int = 0) -> dict:
    key_of = jax.random.split(jax.random.key(seed), 12)
    return {
        "atom_feat": normal_values(key_of[0], (BLOCKS, C, ABLK), 1.0, 6.0, ((0, 128),)),
        "atom_pos": jnp.clip(4.0 * jax.random.uniform(key_of[1], (BLOCKS, 3, ABLK), jnp.float32) ** level_of(key_of[1], (BLOCKS, 3, ABLK), ((0, 128),), -0.2, 0.2), 0.0, 4.0).astype(jnp.bfloat16),
        "atom_counts": plant(jax.random.randint(key_of[2], (BLOCKS,), ABLK // 4, ABLK + 1), jax.random.fold_in(key_of[2], 1), ABLK // 4, ABLK).astype(jnp.int32),
        "atom_nbrs": draw_atom_nbrs(jax.random.fold_in(key_of[11], 71), 0),
        "probe_pos": jnp.clip(4.0 * jax.random.uniform(key_of[4], (TILES, 3, PT), jnp.float32) ** level_of(key_of[4], (TILES, 3, PT), ((0, 128),), -0.2, 0.2), 0.0, 4.0),
        "probe_target": normal_values(key_of[5], (TILES, PT), 1.0, 6.0, ((0, 128),), jnp.float32),
        "tile_blocks": draw_tile_blocks(jax.random.fold_in(key_of[11], 71), 0),
        "atom_filter": normal_values(key_of[7], (C, NRAD * C), C ** -0.5, 0.5),
        "probe_filter": normal_values(key_of[8], (C, NRAD * C), C ** -0.5, 0.5),
        "mix_weight": normal_values(key_of[9], (C, C), C ** -0.5, 0.5),
        "readout": normal_values(key_of[10], (C,), C ** -0.5, 0.5, (), jnp.float32),
    }


CUTOFF = 6.0
SPACING = 0.75
SPREAD = 0.75

def silu_slope(values):
    sigmoid_part = jax.nn.sigmoid(values)
    return sigmoid_part * (1.0 + values * (1.0 - sigmoid_part))

def radial(source, target, factor):
    square = jnp.zeros((source.shape[1], target.shape[1]), source.dtype)
    for component in range(3):
        offset = source[component][:, None] - target[component][None, :]
        square = square + offset * offset
    distance = jnp.sqrt(square + 0.01)
    envelope = jnp.where(distance < CUTOFF, 0.5 * (jnp.cos(jnp.pi * distance / CUTOFF) + 1.0), 0.0)
    centers = jnp.arange(NRAD).astype(source.dtype) * SPACING
    shifted = (distance[None] - centers[:, None, None]) / SPREAD
    return jnp.exp(-shifted * shifted) * (envelope * factor)[None]

def rounded(values):
    narrow = lax.optimization_barrier(values.astype(jnp.bfloat16))
    return narrow.astype(jnp.float32)

def reference(atom_feat, atom_pos, atom_counts, atom_nbrs, probe_pos, probe_target, tile_blocks, atom_filter, probe_filter, mix_weight, readout):
    highest = lax.Precision.HIGHEST
    atom_mask = (jnp.arange(ABLK)[None, :] < atom_counts[:, None]).astype(jnp.float32)
    masked_feat = (atom_feat.astype(jnp.float32) * atom_mask[:, None, :]).astype(jnp.bfloat16)
    coords = atom_pos.astype(jnp.float32)
    atom_scale = (KA * ABLK) ** (-0.5)
    probe_scale = (KB * ABLK) ** (-0.5)

    def atom_block(block_index):
        sources = atom_nbrs[block_index]
        source_feat = masked_feat[sources].astype(jnp.float32)
        target_where = coords[block_index]
        kernel_rows = jax.vmap(lambda source: radial(source, target_where, atom_scale))(coords[sources])
        kernel_rows = rounded(kernel_rows)
        atom_sums = jnp.einsum('kcj,krji->rci', source_feat, kernel_rows)
        atom_sums = atom_sums.astype(jnp.bfloat16).reshape(NRAD * C, ABLK)
        message = jnp.dot(atom_filter, atom_sums, preferred_element_type=jnp.float32)
        updated = ((atom_feat[block_index].astype(jnp.float32) + jax.nn.silu(message)) * atom_mask[block_index][None, :]).astype(jnp.bfloat16)
        return (updated, atom_sums, message)
    updated, atom_sums, message = lax.map(atom_block, jnp.arange(BLOCKS))

    def probe_tile(tile_index):
        read_blocks = tile_blocks[tile_index]
        probe_where = probe_pos[tile_index]

        def kernel_of(block_id):
            return rounded(radial(coords[block_id], probe_where, probe_scale))

        def forward(total_sum, block_id):
            block_term = jnp.einsum('ca,rap->rcp', updated[block_id].astype(jnp.float32), kernel_of(block_id))
            return (total_sum + block_term, None)
        summed, _ = lax.scan(forward, jnp.zeros((NRAD, C, PT), jnp.float32), read_blocks)
        summed = summed.astype(jnp.bfloat16).reshape(NRAD * C, PT)
        hidden = jnp.dot(probe_filter, summed, preferred_element_type=jnp.float32)
        squashed = jax.nn.silu(hidden).astype(jnp.bfloat16)
        mixed_rows = jnp.dot(mix_weight, squashed, preferred_element_type=jnp.float32)
        outer_act = jax.nn.silu(mixed_rows)
        density = jnp.dot(readout, outer_act, precision=highest)
        misfit = (density - probe_target[tile_index]) / PT
        grad_readout = jnp.dot(outer_act, misfit, precision=highest)
        grad_mixed = (readout[:, None] * misfit[None, :] * silu_slope(mixed_rows)).astype(jnp.bfloat16)
        grad_mix = jnp.dot(grad_mixed, squashed.T, preferred_element_type=jnp.float32)
        grad_squashed = jnp.dot(mix_weight.T, grad_mixed, preferred_element_type=jnp.float32)
        grad_hidden = (grad_squashed * silu_slope(hidden)).astype(jnp.bfloat16)
        grad_probe = jnp.dot(grad_hidden, summed.T, preferred_element_type=jnp.float32)
        grad_summed = jnp.dot(probe_filter.T, grad_hidden, preferred_element_type=jnp.float32)
        grad_summed = grad_summed.astype(jnp.bfloat16).astype(jnp.float32).reshape(NRAD, C, PT)

        def backward(block_id):
            return jnp.einsum('rcp,rap->ca', grad_summed, kernel_of(block_id))
        grad_blocks = lax.map(backward, read_blocks)
        return (density, grad_probe, grad_mix, grad_readout, grad_blocks)
    density, grad_probe, grad_mix, grad_readout, grad_blocks = lax.map(probe_tile, jnp.arange(TILES))
    group_count = TILES // TL_DEV
    group_slots = TL_DEV * KB
    group_ids = tile_blocks.reshape(group_count, group_slots)
    group_grads = grad_blocks.reshape(group_count, group_slots, C, ABLK)
    earlier = jnp.tril(jnp.ones((group_slots, group_slots), jnp.float32), -1)

    def group_partial(pair):
        ids_here, grads_here = pair
        same = (ids_here[:, None] == ids_here[None, :]).astype(jnp.float32)
        summed = jnp.einsum('st,tca->sca', same, grads_here, precision=highest)
        repeated = lax.optimization_barrier(jnp.sum(earlier * same, axis=1)) > 0.5
        keep = jnp.where(repeated, 0.0, 1.0).astype(jnp.float32)
        return rounded(summed) * keep[:, None, None]
    partials = lax.map(group_partial, (group_ids, group_grads))
    block_grad = jnp.zeros((BLOCKS, C, ABLK), jnp.float32)
    block_grad = block_grad.at[tile_blocks.reshape(-1)].add(partials.reshape(TILES * KB, C, ABLK))
    grad_message = (block_grad * atom_mask[:, None, :] * silu_slope(message)).astype(jnp.bfloat16)
    atom_filter_grad = jnp.einsum('bca,bda->cd', grad_message.astype(jnp.float32), atom_sums.astype(jnp.float32))
    return (density, atom_filter_grad, lax.optimization_barrier(jnp.sum(grad_probe, axis=0)), lax.optimization_barrier(jnp.sum(grad_mix, axis=0)), lax.optimization_barrier(jnp.sum(grad_readout, axis=0)))
```

```python
import functools
import math

import jax
import jax.numpy as jnp
import numpy as np
from jax import lax
from jax.experimental import pallas as pl
from jax.experimental.pallas import tpu as pltpu
from jax.sharding import PartitionSpec as P

BOTH = ("space", "tile")
F32 = jnp.float32
BF16 = jnp.bfloat16

CUTOFF = 6.0
SPACING = 0.75
SPREAD = 0.75
SOFT = 0.01
AUG = 16
MARK = 32.0


def envelope_terms(degree=4):
    top = CUTOFF * CUTOFF
    nodes = 0.5 * top * (1.0 - np.cos(np.pi * (np.arange(64) + 0.5) / 64))
    values = np.cos(np.pi * np.sqrt(nodes) / (2 * CUTOFF)) / (top - nodes)
    fit = np.polynomial.chebyshev.Chebyshev.fit(nodes, values, degree, domain=[0.0, top])
    return [float(c) for c in fit.convert(kind=np.polynomial.Polynomial).coef]


ENVELOPE = envelope_terms()


def radial_store(square, factor, filters, store):
    distance = square * lax.rsqrt(square)
    root = math.sqrt(factor)
    poly = jnp.full_like(square, ENVELOPE[-1] * root)
    for term in ENVELOPE[-2::-1]:
        poly = poly * square + term * root
    half = jnp.maximum(CUTOFF * CUTOFF - square, 0.0) * poly
    value = (half * half) * jnp.exp2(square * (-math.log2(math.e) / SPREAD**2))
    growth = jnp.exp2(distance * (2.0 * math.log2(math.e) * SPACING / SPREAD**2))
    for r in range(filters):
        store(r, value.astype(BF16))
        if r + 1 < filters:
            value = value * growth


def decay(r):
    return math.exp(-((r * SPACING / SPREAD) ** 2))


def sigmoid(values):
    return 1.0 / (1.0 + jnp.exp(-values))


def dot(a, b, contract):
    return lax.dot_general(a, b, ((contract[0:1], contract[1:2]), ((), ())), preferred_element_type=F32)


def stacked(rows):
    at = lax.broadcasted_iota(jnp.int32, (AUG, rows[0].shape[1]), 0)
    out = jnp.zeros(at.shape, F32)
    for i, row in enumerate(rows):
        out = jnp.where(at == i, row, out)
    return out.astype(BF16)


def pieces(values):
    high = values.astype(BF16).astype(F32)
    rest = values - high
    middle = rest.astype(BF16).astype(F32)
    return [high, middle, rest - middle]


def source_rows(x, y, z):
    unit = jnp.ones_like(x)
    return stacked([x, y, z] * 3 + pieces(x * x + y * y + z * z) + [unit] * 3)


def target_rows(x, y, z):
    unit = jnp.ones_like(x)
    parts = [pieces(-2.0 * row) for row in (x, y, z)]
    rows = [part[i] for i in range(3) for part in parts]
    return stacked(rows + [unit] * 3 + pieces(x * x + y * y + z * z + SOFT))


def setup_kernel(reads_ref, counts_ref, where_ref, early_ref, marked_ref, info_ref, asks):
    peers = early_ref.shape[0]
    blocks = where_ref.shape[1]
    width = where_ref.shape[2]
    tiles, reads = reads_ref.shape
    owners, spots = [], []
    for t in range(tiles):
        for k in range(reads):
            block = reads_ref[t, k]
            owners.append(lax.rem(lax.div(block, blocks), peers))
            spots.append(lax.rem(block, blocks))
    for i in range(2 * peers):
        asks[i] = 0
    for i, (owner, spot) in enumerate(zip(owners, spots)):
        rank = jnp.int32(0)
        for j in range(len(owners)):
            if j != i:
                rank = jnp.where((owners[j] == owner) & (spots[j] < spot), 1, rank)
        slot = owner * 2 + rank
        info_ref[0, i] = slot
        info_ref[1, i] = owner
        info_ref[2, i] = spot
        asks[slot] = spot
    line = lax.broadcasted_iota(jnp.int32, (blocks, width), 0)
    lane = lax.broadcasted_iota(jnp.int32, (blocks, width), 1)
    counts = jnp.zeros((blocks, width), jnp.int32)
    for i in range(blocks):
        counts = jnp.where(line == i, counts_ref[i], counts)
    for c in range(3):
        marked_ref[c] = jnp.where(lane < counts, where_ref[c].astype(F32), 2.0 * MARK).astype(BF16)
    lane = lax.broadcasted_iota(jnp.int32, (AUG, width), 1)
    for t in range(peers):
        for c in range(3):
            early_ref[t, c * blocks : (c + 1) * blocks, :] = where_ref[c]
        note = jnp.where(lane == 0, asks[2 * t], jnp.where(lane == 1, asks[2 * t + 1], 0))
        early_ref[t, 3 * blocks :, :] = note.astype(F32).astype(BF16)


def atom_kernel(peers, nbr_ref, lo_ref, own_ref, hi_ref, lo_pos, own_pos, hi_pos, weight_ref,
                sums_ref, slope_ref, done_ref, rows, masks, goals, feat, kern):
    b = pl.program_id(0)
    blocks, channels, width = own_ref.shape
    nbrs = feat.shape[1]
    filters = kern.shape[1]
    scale = (nbrs * width) ** -0.5

    @pl.when(b == 0)
    def _():
        for s, pos in enumerate((lo_pos, own_pos, hi_pos)):
            wide = [pos[c].astype(F32) for c in range(3)]
            there = wide[0] < MARK
            wide = [jnp.where(there, w, 0.0) for w in wide]
            masks[s] = there.astype(F32)
            for i in range(blocks):
                x, y, z = (w[i : i + 1, :] for w in wide)
                rows[s * blocks + i] = source_rows(x, y, z)
                if s == 1:
                    goals[i] = target_rows(x, y, z)

    def pick(slot, k, feats, s, index):
        mask = jnp.broadcast_to(masks[s, pl.ds(index, 1), :], (channels, width)).astype(BF16)
        feat[slot, k] = feats[index] * mask

    def prepare(slot, k, index):
        square = dot(rows[index], goals[jnp.minimum(b, blocks - 1)], (0, 0))

        def store(r, value):
            kern[slot, r, k * width : (k + 1) * width, :] = value

        radial_store(square, scale, filters, store)

    def finish(slot, r):
        feats = jnp.concatenate([feat[slot, k] for k in range(nbrs)], axis=1)
        kerns = jnp.concatenate([kern[slot, r], kern[slot, r + 1]], axis=1)
        part = dot(feats, kerns, (1, 0))
        for i in range(2):
            piece = part[:, i * width : (i + 1) * width] * decay(r + i)
            sums_ref[0, (r + i) * channels : (r + i + 1) * channels, :] = piece.astype(BF16)

    def last(at):
        sums = sums_ref[0]
        message = dot(weight_ref[...], sums, (1, 0))
        mask = masks[1, pl.ds(at, 1), :]
        gate = sigmoid(message)
        slope_ref[0] = gate * (1.0 + message * (1.0 - gate)) * mask
        done_ref[0] = ((own_ref[at].astype(F32) + message * gate) * mask).astype(BF16)

    def step(slot):
        at = jnp.minimum(b, blocks - 1)
        picked = [nbr_ref[k, at] for k in range(nbrs)]
        index = [lax.rem(block, blocks) for block in picked]
        space = [lax.div(block, blocks * peers) for block in picked]
        side = jnp.where(space[3] == space[2], 1, jnp.where(space[3] == space[0], 0, 2))
        sides = [0, 2, 1, side]
        pick(slot, 0, lo_ref, 0, index[0])
        pick(slot, 1, hi_ref, 2, index[1])
        pick(slot, 2, own_ref, 1, index[2])
        for s, feats in enumerate((lo_ref, own_ref, hi_ref)):
            @pl.when(side == s)
            def _():
                pick(slot, 3, feats, s, index[3])

        for k in range(nbrs):
            prepare(slot, k, sides[k] * blocks + index[k])
            finish(1 - slot, 2 * k)
        last(jnp.maximum(b - 1, 0))

    @pl.when(b % 2 == 0)
    def _():
        step(0)

    @pl.when(b % 2 == 1)
    def _():
        step(1)


def radial_kernel(info_ref, early_ref, probe_ref, kern_ref, places, goals):
    b = pl.program_id(0)
    blocks = (early_ref.shape[1] - AUG) // 3
    width = early_ref.shape[2]
    chunks = kern_ref.shape[2]
    filters = kern_ref.shape[1]
    reads = pl.num_programs(0) // probe_ref.shape[1]
    scale = (reads * width) ** -0.5

    @pl.when(b == 0)
    def _():
        places[...] = early_ref[...].astype(F32)
        for t in range(probe_ref.shape[1]):
            goals[t] = target_rows(*(probe_ref[c, t : t + 1, :] for c in range(3)))

    owner, spot = info_ref[1, b], info_ref[2, b]
    rows = source_rows(*(places[owner, pl.ds(c * blocks + spot, 1), :] for c in range(3)))
    goal = goals[b // reads]
    for at in range(chunks):
        square = dot(rows, goal[:, at * 128 : (at + 1) * 128], (0, 0))

        def store(r, value):
            kern_ref[0, r, at] = value

        radial_store(square, scale, filters, store)


def probe_kernel(info_ref, reply_ref, kern_ref, goal_ref, weight_ref, mix_ref, read_ref,
                 density_ref, probe_ref, mixg_ref, readg_ref, back_ref, held, arrived, sums, grads, total):
    t = pl.program_id(0)
    slots, channels, width = reply_ref.shape
    filters, chunks = held.shape[1:3]
    reads = held.shape[3] // width
    probes = goal_ref.shape[1]

    def fetch(at, r):
        return pltpu.make_async_copy(kern_ref.at[at, r], held.at[at, r], arrived.at[at, r])

    @pl.when(t == 0)
    def _():
        for at in range(held.shape[0]):
            for r in range(filters):
                fetch(at, r).start()
        total[...] = jnp.zeros_like(total)
        probe_ref[...] = jnp.zeros_like(probe_ref)
        mixg_ref[...] = jnp.zeros_like(mixg_ref)
        readg_ref[...] = jnp.zeros_like(readg_ref)

    feats = jnp.concatenate([reply_ref[info_ref[0, t * reads + k]] for k in range(reads)], axis=1)
    for r in range(filters):
        fetch(t, r).wait()
        for at in range(0, chunks, 2):
            kerns = jnp.concatenate([held[t, r, at], held[t, r, at + 1]], axis=1)
            part = (dot(feats, kerns, (1, 0)) * decay(r)).astype(BF16)
            for i in range(2):
                sums[at + i, r * channels : (r + 1) * channels, :] = part[:, i * 128 : (i + 1) * 128]
    all_sums = jnp.concatenate([sums[at] for at in range(chunks)], axis=1)
    hidden = dot(weight_ref[...], all_sums, (1, 0))
    gate = sigmoid(hidden)
    squashed = (hidden * gate).astype(BF16)
    hidden_slope = gate * (1.0 + hidden * (1.0 - gate))
    mixed = dot(mix_ref[...], squashed, (1, 0))
    outer_gate = sigmoid(mixed)
    outer = mixed * outer_gate
    line = lax.broadcasted_iota(jnp.int32, (channels, channels), 0)
    diagonal = line == lax.broadcasted_iota(jnp.int32, (channels, channels), 1)
    readout = jnp.sum(jnp.where(diagonal, read_ref[...], 0.0), axis=1, keepdims=True)
    density = jnp.sum(readout * outer, axis=0, keepdims=True)
    density_ref[pl.ds(t, 1), :] = density
    misfit = (density - goal_ref[pl.ds(t, 1), :]) * (1.0 / probes)
    grad_read = jnp.sum(outer * misfit, axis=1, keepdims=True)
    readg_ref[...] += jnp.sum(jnp.where(diagonal, grad_read, 0.0), axis=0, keepdims=True)
    grad_mixed = (readout * misfit * (outer_gate * (1.0 + mixed * (1.0 - outer_gate)))).astype(BF16)
    mixg_ref[...] += dot(grad_mixed, squashed, (1, 1))
    grad_hidden = (dot(mix_ref[...], grad_mixed, (0, 0)) * hidden_slope).astype(BF16)
    probe_ref[...] += dot(grad_hidden, all_sums, (1, 1))
    for r in range(filters):
        part = (dot(weight_ref[:, r * channels : (r + 1) * channels], grad_hidden, (0, 0)) * decay(r)).astype(BF16)
        for at in range(chunks):
            grads[r * chunks + at] = part[:, at * 128 : (at + 1) * 128]
    all_grads = jnp.concatenate([grads[i] for i in range(filters * chunks)], axis=1)
    for k in range(0, reads, 2):
        kerns = jnp.concatenate(
            [held[t, r, at, k * width : (k + 2) * width, :] for r in range(filters) for at in range(chunks)], axis=1
        )
        part = dot(all_grads, kerns, (1, 1))
        for i in range(2):
            slot = info_ref[0, t * reads + k + i]
            total[slot] += part[:, i * width : (i + 1) * width]

    @pl.when(t == pl.num_programs(0) - 1)
    def _():
        back_ref[...] = total[...].astype(BF16)


def owner_kernel(asked_ref, back_ref, slope_ref, sums_ref, probe_ref, mix_ref, read_ref, out_ref, total, grads):
    step = pl.program_id(0)
    blocks, channels, width = slope_ref.shape
    columns = sums_ref.shape[1]
    across = probe_ref.shape[1] // width
    high = 8

    @pl.when(step == 0)
    def _():
        total[...] = jnp.zeros_like(total)

        def gather(i, carry):
            at = asked_ref[i]
            total[at] = total[at] + back_ref[i].astype(F32)
            return carry

        lax.fori_loop(0, back_ref.shape[0], gather, 0)
        for b in range(blocks):
            grads[b] = (total[b] * slope_ref[b]).astype(BF16)
        for i in range(channels // high):
            lines = slice(i * high, (i + 1) * high)
            for j in range(across):
                out_ref[i * across + j, high : 2 * high, :] = probe_ref[lines, j * width : (j + 1) * width].astype(BF16)
            out_ref[i, 2 * high :, :] = mix_ref[lines, :].astype(BF16)
        out_ref[channels // high, 2 * high :, :] = jnp.broadcast_to(read_ref[...], (high, width)).astype(BF16)
        for i in range(channels // high + 1, out_ref.shape[0]):
            out_ref[i, 2 * high :, :] = jnp.zeros((high, width), BF16)

    all_grads = jnp.concatenate([grads[b] for b in range(blocks)], axis=1)
    all_sums = jnp.concatenate([sums_ref[b] for b in range(blocks)], axis=1)
    part = dot(all_grads, all_sums, (1, 1)).astype(BF16)
    for i in range(channels // high):
        for j in range(columns // width):
            out_ref[i * across + step * (columns // width) + j, :high, :] = part[
                i * high : (i + 1) * high, j * width : (j + 1) * width
            ]


def spread_kernel(parts_ref, out_ref):
    mine = jnp.sum(parts_ref[...].astype(F32), axis=0, keepdims=True).astype(BF16)
    out_ref[...] = jnp.broadcast_to(mine, out_ref.shape)


def whole(shape):
    return pl.BlockSpec(shape, lambda *_: (0,) * len(shape))


def one(shape):
    return pl.BlockSpec((1, *shape[1:]), lambda b, *_: (b,) + (0,) * (len(shape) - 1))


def call(kernel, grid, prefetch, ins, in_specs, outs, out_specs, scratch, name, cost, limit=None):
    return pl.pallas_call(
        kernel,
        grid_spec=pltpu.PrefetchScalarGridSpec(
            num_scalar_prefetch=len(prefetch), grid=grid, in_specs=in_specs, out_specs=out_specs,
            scratch_shapes=scratch,
        ),
        out_shape=outs,
        name=name,
        cost_estimate=pl.CostEstimate(flops=cost[0], bytes_accessed=cost[1], transcendentals=cost[2]),
        compiler_params=pltpu.CompilerParams(vmem_limit_bytes=limit),
    )(*prefetch, *ins)


def reduced(chunks):
    sent = lax.all_to_all(chunks, BOTH, 0, 0, tiled=True)
    vmem = pl.BlockSpec(memory_space=pltpu.VMEM)
    totals = pl.pallas_call(
        spread_kernel, in_specs=[vmem], out_specs=vmem, out_shape=jax.ShapeDtypeStruct(sent.shape, BF16), name="spread",
        compiler_params=pltpu.CompilerParams(vmem_limit_bytes=4 << 20),
    )(sent)
    return lax.all_to_all(totals, BOTH, 0, 0, tiled=True)


def body(atom_feat, atom_pos, atom_counts, atom_nbrs, probe_pos, probe_target, tile_blocks, atom_filter, probe_filter,
         mix_weight, readout):
    blocks, channels, width = atom_feat.shape
    tiles, reads = tile_blocks.shape
    probes = probe_pos.shape[2]
    chunks = probes // 128
    filters = atom_filter.shape[1] // channels
    peers = lax.axis_size("tile")
    spaces = lax.axis_size("space")
    devices = peers * spaces
    slots = peers * 2
    up = [(i, (i + 1) % spaces) for i in range(spaces)]
    down = [(i, (i - 1) % spaces) for i in range(spaces)]

    feat_lo = lax.ppermute(atom_feat, "space", up)
    feat_hi = lax.ppermute(atom_feat, "space", down)
    smem = pl.BlockSpec(memory_space=pltpu.SMEM)
    vmem = pl.BlockSpec(memory_space=pltpu.VMEM)
    where = jnp.transpose(atom_pos, (1, 0, 2))
    early, marked, info = pl.pallas_call(
        setup_kernel,
        in_specs=[smem, smem, vmem],
        out_specs=[vmem, vmem, smem],
        out_shape=(
            jax.ShapeDtypeStruct((peers, 3 * blocks + AUG, width), BF16),
            jax.ShapeDtypeStruct(where.shape, BF16),
            jax.ShapeDtypeStruct((3, tiles * reads), jnp.int32),
        ),
        scratch_shapes=[pltpu.SMEM((slots,), jnp.int32)],
        name="requests",
        compiler_params=pltpu.CompilerParams(vmem_limit_bytes=4 << 20),
    )(tile_blocks, atom_counts, where)
    pos_lo = lax.ppermute(marked, "space", up)
    pos_hi = lax.ppermute(marked, "space", down)
    early = lax.all_to_all(early, "tile", 0, 0, tiled=True)

    pairs = blocks * 4 * width * width

    def before(shape):
        return pl.BlockSpec((1, *shape[1:]), lambda b, *_: (jnp.maximum(b - 1, 0),) + (0,) * (len(shape) - 1))

    sums_shape = (blocks, filters * channels, width)
    sums, slope, done = call(
        functools.partial(atom_kernel, peers), (blocks + 1,), (atom_nbrs.T,),
        (feat_lo, atom_feat, feat_hi, pos_lo, marked, pos_hi, atom_filter),
        [whole(atom_feat.shape)] * 3 + [whole(marked.shape)] * 3 + [whole(atom_filter.shape)],
        (
            jax.ShapeDtypeStruct(sums_shape, BF16),
            jax.ShapeDtypeStruct(atom_feat.shape, F32),
            jax.ShapeDtypeStruct(atom_feat.shape, BF16),
        ),
        [before(sums_shape), before(atom_feat.shape), before(atom_feat.shape)],
        [
            pltpu.VMEM((3 * blocks, AUG, width), BF16),
            pltpu.VMEM((3, blocks, width), F32),
            pltpu.VMEM((blocks, AUG, width), BF16),
            pltpu.VMEM((2, 4, channels, width), BF16),
            pltpu.VMEM((2, filters, 4 * width, width), BF16),
        ],
        "atom_layer", (2 * pairs * filters * channels, 8 << 20, 3 * pairs), 49 << 20,
    )
    asked = early[:, blocks * 3, :2].astype(jnp.int32).reshape(slots)
    sent = done.at[asked].get(mode="promise_in_bounds")
    replies = lax.all_to_all(
        sent.reshape(peers, 2 * channels, width), "tile", 0, 0, tiled=True
    ).reshape(slots, channels, width)

    pairs = tiles * reads * width * probes
    kern_shape = (tiles, filters, chunks, reads * width, 128)
    kern = call(
        radial_kernel, (tiles * reads,), (info,), (early, jnp.transpose(probe_pos, (1, 0, 2))),
        [whole(early.shape), whole((3, tiles, probes))],
        jax.ShapeDtypeStruct(kern_shape, BF16),
        pl.BlockSpec((1, filters, chunks, width, 128), lambda b, *_: (b // reads, 0, 0, b % reads, 0)),
        [pltpu.VMEM(early.shape, F32), pltpu.VMEM((tiles, AUG, probes), BF16)],
        "probe_filters", (40 * pairs, 2 * filters * pairs, 3 * pairs), 50 << 20,
    )
    flat = (tiles, probes)
    density, grad_probe, grad_mix, grad_read, back = call(
        probe_kernel, (tiles,), (info,),
        (replies, kern, probe_target, probe_filter, mix_weight, readout.reshape(1, channels)),
        [whole(replies.shape), pl.BlockSpec(memory_space=pl.ANY), whole(flat), whole(probe_filter.shape), whole(mix_weight.shape),
         whole((1, channels))],
        (
            jax.ShapeDtypeStruct(flat, F32),
            jax.ShapeDtypeStruct(probe_filter.shape, F32),
            jax.ShapeDtypeStruct(mix_weight.shape, F32),
            jax.ShapeDtypeStruct((1, channels), F32),
            jax.ShapeDtypeStruct(replies.shape, BF16),
        ),
        [whole(flat), whole(probe_filter.shape), whole(mix_weight.shape), whole((1, channels)), whole(replies.shape)],
        [
            pltpu.VMEM(kern_shape, BF16),
            pltpu.SemaphoreType.DMA((tiles, filters)),
            pltpu.VMEM((chunks, filters * channels, 128), BF16),
            pltpu.VMEM((filters * chunks, channels, 128), BF16),
            pltpu.VMEM(replies.shape, F32),
        ],
        "probe_layer", (4 * pairs * filters * channels, 20 << 20, 0), 50 << 20,
    )
    returned = lax.all_to_all(
        back.reshape(peers, 2 * channels, width), "tile", 0, 0, tiled=True
    ).reshape(slots, channels, width)

    columns = 256
    part_shape = (devices, 24, width)
    parts = call(
        owner_kernel, (filters * channels // columns,), (asked,),
        (returned, slope, sums, grad_probe, grad_mix, grad_read),
        [whole(returned.shape), whole(slope.shape), pl.BlockSpec((blocks, columns, width), lambda j, *_: (0, j, 0)),
         whole(grad_probe.shape), whole(grad_mix.shape), whole((1, channels))],
        jax.ShapeDtypeStruct(part_shape, BF16), whole(part_shape),
        [pltpu.VMEM(slope.shape, F32), pltpu.VMEM(slope.shape, BF16)], "atom_gradient",
        (2 * blocks * width * channels * filters * channels, 8 << 20, 0), 49 << 20,
    )
    sums = reduced(parts)

    def filter_of(tiled):
        tall = tiled.reshape(channels // 8, filters, 8, channels)
        return jnp.transpose(tall, (0, 2, 1, 3)).reshape(channels, filters * channels).astype(F32)

    return (
        density,
        filter_of(sums[:, :8]),
        filter_of(sums[:, 8:16]),
        sums[: channels // 8, 16:].reshape(channels, channels).astype(F32),
        sums[channels // 8, 16].astype(F32),
    )


def solution(mesh):
    split2 = P(BOTH, None)
    split3d = P(BOTH, None, None)
    in_specs = (split3d, split3d, P(BOTH), split2, split3d, split2, split2, P(), P(), P(), P())
    out_specs = (split2, P(), P(), P(), P())
    return jax.shard_map(body, mesh=mesh, in_specs=in_specs, out_specs=out_specs, check_vma=False)
```

```python
import functools
import math

import jax
import jax.numpy as jnp
import numpy as np
from jax import lax
from jax.experimental import pallas as pl
from jax.experimental.pallas import tpu as pltpu
from jax.sharding import PartitionSpec as P

BOTH = ("space", "tile")
F32 = jnp.float32
BF16 = jnp.bfloat16

CUTOFF = 6.0
SPACING = 0.75
SPREAD = 0.75
SOFT = 0.01
AUG = 16
READY = 5
MARK = 32.0


def envelope_terms(degree=4):
    top = CUTOFF * CUTOFF
    nodes = 0.5 * top * (1.0 - np.cos(np.pi * (np.arange(64) + 0.5) / 64))
    values = np.cos(np.pi * np.sqrt(nodes) / (2 * CUTOFF)) / (top - nodes)
    fit = np.polynomial.chebyshev.Chebyshev.fit(nodes, values, degree, domain=[0.0, top])
    return [float(c) for c in fit.convert(kind=np.polynomial.Polynomial).coef]


ENVELOPE = envelope_terms()


def radial_store(square, factor, filters, store):
    distance = square * lax.rsqrt(square)
    root = math.sqrt(factor)
    poly = jnp.full_like(square, ENVELOPE[-1] * root)
    for term in ENVELOPE[-2::-1]:
        poly = poly * square + term * root
    half = jnp.maximum(CUTOFF * CUTOFF - square, 0.0) * poly
    value = (half * half) * jnp.exp2(square * (-math.log2(math.e) / SPREAD**2))
    growth = jnp.exp2(distance * (2.0 * math.log2(math.e) * SPACING / SPREAD**2))
    for r in range(filters):
        store(r, value.astype(BF16))
        if r + 1 < filters:
            value = value * growth


def decay(r):
    return math.exp(-((r * SPACING / SPREAD) ** 2))


def sigmoid(values):
    return 1.0 / (1.0 + jnp.exp(-values))


def dot(a, b, contract):
    return lax.dot_general(a, b, ((contract[0:1], contract[1:2]), ((), ())), preferred_element_type=F32)


def stacked(rows):
    at = lax.broadcasted_iota(jnp.int32, (AUG, rows[0].shape[1]), 0)
    out = jnp.zeros(at.shape, F32)
    for i, row in enumerate(rows):
        out = jnp.where(at == i, row, out)
    return out.astype(BF16)


def pieces(values):
    high = values.astype(BF16).astype(F32)
    rest = values - high
    middle = rest.astype(BF16).astype(F32)
    return [high, middle, rest - middle]


def source_rows(x, y, z):
    unit = jnp.ones_like(x)
    return stacked([x, y, z] * 3 + pieces(x * x + y * y + z * z) + [unit] * 3)


def target_rows(x, y, z):
    unit = jnp.ones_like(x)
    parts = [pieces(-2.0 * row) for row in (x, y, z)]
    rows = [part[i] for i in range(3) for part in parts]
    return stacked(rows + [unit] * 3 + pieces(x * x + y * y + z * z + SOFT))


def setup_kernel(reads_ref, counts_ref, where_ref, early_ref, marked_ref, info_ref, asks):
    peers = early_ref.shape[0]
    blocks = where_ref.shape[1]
    width = where_ref.shape[2]
    tiles, reads = reads_ref.shape
    owners, spots = [], []
    for t in range(tiles):
        for k in range(reads):
            block = reads_ref[t, k]
            owners.append(lax.rem(lax.div(block, blocks), peers))
            spots.append(lax.rem(block, blocks))
    for i in range(2 * peers):
        asks[i] = 0
    for i, (owner, spot) in enumerate(zip(owners, spots)):
        rank = jnp.int32(0)
        for j in range(len(owners)):
            if j != i:
                rank = jnp.where((owners[j] == owner) & (spots[j] < spot), 1, rank)
        slot = owner * 2 + rank
        info_ref[0, i] = slot
        info_ref[1, i] = owner
        info_ref[2, i] = spot
        asks[slot] = spot
    line = lax.broadcasted_iota(jnp.int32, (blocks, width), 0)
    lane = lax.broadcasted_iota(jnp.int32, (blocks, width), 1)
    counts = jnp.zeros((blocks, width), jnp.int32)
    for i in range(blocks):
        counts = jnp.where(line == i, counts_ref[i], counts)
    for c in range(3):
        marked_ref[c] = jnp.where(lane < counts, where_ref[c].astype(F32), 2.0 * MARK).astype(BF16)
    lane = lax.broadcasted_iota(jnp.int32, (AUG, width), 1)
    for t in range(peers):
        for c in range(3):
            early_ref[t, c * blocks : (c + 1) * blocks, :] = where_ref[c]
        note = jnp.where(lane == 0, asks[2 * t], jnp.where(lane == 1, asks[2 * t + 1], 0))
        early_ref[t, 3 * blocks :, :] = note.astype(F32).astype(BF16)


def atom_kernel(peers, nbr_ref, lo_ref, own_ref, hi_ref, lo_pos, own_pos, hi_pos, weight_ref,
                sums_ref, slope_ref, done_ref, rows, masks, goals, feat, kern):
    b = pl.program_id(0)
    blocks, channels, width = own_ref.shape
    nbrs = feat.shape[1]
    filters = kern.shape[1]
    scale = (nbrs * width) ** -0.5

    @pl.when(b == 0)
    def _():
        for s, pos in enumerate((lo_pos, own_pos, hi_pos)):
            wide = [pos[c].astype(F32) for c in range(3)]
            there = wide[0] < MARK
            wide = [jnp.where(there, w, 0.0) for w in wide]
            masks[s] = there.astype(F32)
            for i in range(blocks):
                x, y, z = (w[i : i + 1, :] for w in wide)
                rows[s * blocks + i] = source_rows(x, y, z)
                if s == 1:
                    goals[i] = target_rows(x, y, z)

    def pick(slot, k, feats, s, index):
        mask = jnp.broadcast_to(masks[s, pl.ds(index, 1), :], (channels, width)).astype(BF16)
        feat[slot, k] = feats[index] * mask

    def prepare(slot, k, index):
        square = dot(rows[index], goals[jnp.minimum(b, blocks - 1)], (0, 0))

        def store(r, value):
            kern[slot, r, k * width : (k + 1) * width, :] = value

        radial_store(square, scale, filters, store)

    def finish(slot, r):
        feats = jnp.concatenate([feat[slot, k] for k in range(nbrs)], axis=1)
        kerns = jnp.concatenate([kern[slot, r], kern[slot, r + 1]], axis=1)
        part = dot(feats, kerns, (1, 0))
        for i in range(2):
            piece = part[:, i * width : (i + 1) * width] * decay(r + i)
            sums_ref[0, (r + i) * channels : (r + i + 1) * channels, :] = piece.astype(BF16)

    def last(at):
        sums = sums_ref[0]
        message = dot(weight_ref[...], sums, (1, 0))
        mask = masks[1, pl.ds(at, 1), :]
        gate = sigmoid(message)
        slope_ref[0] = gate * (1.0 + message * (1.0 - gate)) * mask
        done_ref[0] = ((own_ref[at].astype(F32) + message * gate) * mask).astype(BF16)

    def step(slot):
        at = jnp.minimum(b, blocks - 1)
        picked = [nbr_ref[k, at] for k in range(nbrs)]
        index = [lax.rem(block, blocks) for block in picked]
        space = [lax.div(block, blocks * peers) for block in picked]
        side = jnp.where(space[3] == space[2], 1, jnp.where(space[3] == space[0], 0, 2))
        sides = [0, 2, 1, side]
        pick(slot, 0, lo_ref, 0, index[0])
        pick(slot, 1, hi_ref, 2, index[1])
        pick(slot, 2, own_ref, 1, index[2])
        for s, feats in enumerate((lo_ref, own_ref, hi_ref)):
            @pl.when(side == s)
            def _():
                pick(slot, 3, feats, s, index[3])

        for k in range(nbrs):
            prepare(slot, k, sides[k] * blocks + index[k])
            finish(1 - slot, 2 * k)
        last(jnp.maximum(b - 1, 0))

    @pl.when(b % 2 == 0)
    def _():
        step(0)

    @pl.when(b % 2 == 1)
    def _():
        step(1)


def radial_block(rows, goals_ref, t, scale, filters, store):
    for at in range(goals_ref.shape[1]):
        square = dot(rows, goals_ref[t, at], (0, 0))
        radial_store(square, scale, filters, functools.partial(store, at))


def rows_kernel(info_ref, early_ref, probe_ref, rows_ref, goals_ref, kern_ref, places, held, left):
    blocks = (early_ref.shape[1] - AUG) // 3
    width = early_ref.shape[2]
    reads = rows_ref.shape[0] // goals_ref.shape[0]
    scale = (reads * width) ** -0.5
    places[...] = early_ref[...].astype(F32)
    for b in range(rows_ref.shape[0]):
        owner, spot = info_ref[1, b], info_ref[2, b]
        rows_ref[b] = source_rows(*(places[owner, pl.ds(c * blocks + spot, 1), :] for c in range(3)))
    for t in range(goals_ref.shape[0]):
        goal = target_rows(*(probe_ref[c, t : t + 1, :] for c in range(3)))
        for at in range(goals_ref.shape[1]):
            goals_ref[t, at] = goal[:, at * 128 : (at + 1) * 128]

    def leave(k):
        return pltpu.make_async_copy(held.at[k], kern_ref.at[k], left.at[k])

    for k in range(held.shape[0]):
        def store(at, r, value):
            held[k, r, at] = value

        radial_block(rows_ref[k], goals_ref, 0, scale, held.shape[1], store)
        leave(k).start()
    for k in range(held.shape[0]):
        leave(k).wait()


def probe_kernel(info_ref, ready_ref, rows_ref, goals_ref, reply_ref, goal_ref, weight_ref, mix_ref, read_ref,
                 density_ref, probe_ref, mixg_ref, readg_ref, back_ref,
                 first, second, arrived, sums, squashed, grads_mixed, grads_hidden, slopes, grads, total):
    _, channels, width = reply_ref.shape
    tiles, probes = goal_ref.shape
    filters, chunks = first.shape[:2]
    reads = rows_ref.shape[0] // tiles
    ready = ready_ref.shape[0]
    scale = (reads * width) ** -0.5
    kerns = (first, second)

    def fetch(k):
        return pltpu.make_async_copy(ready_ref.at[k], first.at[:, :, k * width : (k + 1) * width, :], arrived.at[k])

    for k in range(ready):
        fetch(k).start()
    line = lax.broadcasted_iota(jnp.int32, (channels, channels), 0)
    diagonal = line == lax.broadcasted_iota(jnp.int32, (channels, channels), 1)
    readout = jnp.sum(jnp.where(diagonal, read_ref[...], 0.0), axis=1, keepdims=True)
    total[...] = jnp.zeros_like(total)

    def radial(t, k):
        def store(at, r, value):
            kerns[t][r, at, pl.ds(pl.multiple_of(k * width, width), width), :] = value

        radial_block(rows_ref[t * reads + k], goals_ref, t, scale, filters, store)

    def forward(t):
        feats = jnp.concatenate([reply_ref[info_ref[0, t * reads + k]] for k in range(reads)], axis=1)
        for r in range(filters):
            for at in range(0, chunks, 2):
                right = jnp.concatenate([kerns[t][r, at], kerns[t][r, at + 1]], axis=1)
                part = (dot(feats, right, (1, 0)) * decay(r)).astype(BF16)
                for i in range(2):
                    sums[at + i, r * channels : (r + 1) * channels, :] = part[:, i * 128 : (i + 1) * 128]

    def halves(ref, at, value):
        for i in range(2):
            ref[at + i] = value[:, i * 128 : (i + 1) * 128]

    def middle(t):
        grad_read = jnp.zeros((channels, 1), F32)
        for at in range(0, chunks, 2):
            span = slice(at * 128, (at + 2) * 128)
            hidden = dot(weight_ref[...], jnp.concatenate([sums[at], sums[at + 1]], axis=1), (1, 0))
            gate = sigmoid(hidden)
            squash = (hidden * gate).astype(BF16)
            halves(squashed, at, squash)
            slopes[...] = gate * (1.0 + hidden * (1.0 - gate))
            mixed = dot(mix_ref[...], squash, (1, 0))
            outer_gate = sigmoid(mixed)
            outer = mixed * outer_gate
            density = jnp.sum(readout * outer, axis=0, keepdims=True)
            density_ref[t : t + 1, span] = density
            misfit = (density - goal_ref[t : t + 1, span]) * (1.0 / probes)
            grad_read = grad_read + jnp.sum(outer * misfit, axis=1, keepdims=True)
            grad_mixed = (readout * misfit * (outer_gate * (1.0 + mixed * (1.0 - outer_gate)))).astype(BF16)
            halves(grads_mixed, at, grad_mixed)
            halves(grads_hidden, at, (dot(mix_ref[...], grad_mixed, (0, 0)) * slopes[...]).astype(BF16))
        grad_read = jnp.sum(jnp.where(diagonal, grad_read, 0.0), axis=0, keepdims=True)

        def joined(ref):
            return jnp.concatenate([ref[at] for at in range(chunks)], axis=1)

        grad_hidden = joined(grads_hidden)
        grad_mix = dot(joined(grads_mixed), joined(squashed), (1, 1))
        grad_probe = dot(grad_hidden, joined(sums), (1, 1))
        if t == 0:
            readg_ref[...], mixg_ref[...], probe_ref[...] = grad_read, grad_mix, grad_probe
        else:
            readg_ref[...] += grad_read
            mixg_ref[...] += grad_mix
            probe_ref[...] += grad_probe
        for r in range(filters):
            part = dot(weight_ref[:, r * channels : (r + 1) * channels], grad_hidden, (0, 0)) * decay(r)
            part = part.astype(BF16)
            for at in range(chunks):
                grads[r * chunks + at] = part[:, at * 128 : (at + 1) * 128]

    def backward(t):
        all_grads = jnp.concatenate([grads[i] for i in range(filters * chunks)], axis=1)
        for k in range(0, reads, 2):
            lines = slice(k * width, (k + 2) * width)
            right = jnp.concatenate(
                [kerns[t][r, at, lines, :] for r in range(filters) for at in range(chunks)], axis=1
            )
            part = dot(all_grads, right, (1, 1))
            for i in range(2):
                slot = info_ref[0, t * reads + k + i]
                total[slot] += part[:, i * width : (i + 1) * width]

    @pl.loop(0, reads)
    def _(k):
        radial(1, k)

    @pl.loop(ready, reads)
    def _(k):
        radial(0, k)

    for k in range(ready):
        fetch(k).wait()
    for t in range(tiles):
        forward(t)
        middle(t)
        backward(t)
    back_ref[...] = total[...].astype(BF16)


def owner_kernel(asked_ref, back_ref, slope_ref, sums_ref, probe_ref, mix_ref, read_ref, out_ref, total, grads):
    step = pl.program_id(0)
    blocks, channels, width = slope_ref.shape
    columns = sums_ref.shape[1]
    across = probe_ref.shape[1] // width
    high = 8

    @pl.when(step == 0)
    def _():
        total[...] = jnp.zeros_like(total)

        def gather(i, carry):
            at = asked_ref[i]
            total[at] = total[at] + back_ref[i].astype(F32)
            return carry

        lax.fori_loop(0, back_ref.shape[0], gather, 0)
        for b in range(blocks):
            grads[b] = (total[b] * slope_ref[b]).astype(BF16)
        for i in range(channels // high):
            lines = slice(i * high, (i + 1) * high)
            for j in range(across):
                out_ref[i * across + j, high : 2 * high, :] = probe_ref[lines, j * width : (j + 1) * width].astype(BF16)
            out_ref[i, 2 * high :, :] = mix_ref[lines, :].astype(BF16)
        out_ref[channels // high, 2 * high :, :] = jnp.broadcast_to(read_ref[...], (high, width)).astype(BF16)
        for i in range(channels // high + 1, out_ref.shape[0]):
            out_ref[i, 2 * high :, :] = jnp.zeros((high, width), BF16)

    all_grads = jnp.concatenate([grads[b] for b in range(blocks)], axis=1)
    all_sums = jnp.concatenate([sums_ref[b] for b in range(blocks)], axis=1)
    part = dot(all_grads, all_sums, (1, 1)).astype(BF16)
    for i in range(channels // high):
        for j in range(columns // width):
            out_ref[i * across + step * (columns // width) + j, :high, :] = part[
                i * high : (i + 1) * high, j * width : (j + 1) * width
            ]


def spread_kernel(parts_ref, out_ref):
    mine = jnp.sum(parts_ref[...].astype(F32), axis=0, keepdims=True).astype(BF16)
    out_ref[...] = jnp.broadcast_to(mine, out_ref.shape)


def whole(shape):
    return pl.BlockSpec(shape, lambda *_: (0,) * len(shape))


def call(kernel, grid, prefetch, ins, in_specs, outs, out_specs, scratch, cost, limit=None):
    return pl.pallas_call(
        kernel,
        grid_spec=pltpu.PrefetchScalarGridSpec(
            num_scalar_prefetch=len(prefetch), grid=grid, in_specs=in_specs, out_specs=out_specs,
            scratch_shapes=scratch,
        ),
        out_shape=outs,
        cost_estimate=pl.CostEstimate(flops=cost[0], bytes_accessed=cost[1], transcendentals=cost[2]),
        compiler_params=pltpu.CompilerParams(vmem_limit_bytes=limit),
    )(*prefetch, *ins)


SMEM = pl.BlockSpec(memory_space=pltpu.SMEM)
VMEM = pl.BlockSpec(memory_space=pltpu.VMEM)


def plain(kernel, ins, in_specs, out_specs, outs, scratch, limit, cost=None):
    return pl.pallas_call(
        kernel, in_specs=in_specs, out_specs=out_specs, out_shape=outs, scratch_shapes=scratch,
        cost_estimate=cost and pl.CostEstimate(flops=cost[0], bytes_accessed=cost[1], transcendentals=cost[2]),
        compiler_params=pltpu.CompilerParams(vmem_limit_bytes=limit),
    )(*ins)


def reduced(chunks):
    sent = lax.all_to_all(chunks, BOTH, 0, 0, tiled=True)
    vmem = pl.BlockSpec(memory_space=pltpu.VMEM)
    totals = pl.pallas_call(
        spread_kernel, in_specs=[vmem], out_specs=vmem, out_shape=jax.ShapeDtypeStruct(sent.shape, BF16), name="spread",
        compiler_params=pltpu.CompilerParams(vmem_limit_bytes=4 << 20),
    )(sent)
    return lax.all_to_all(totals, BOTH, 0, 0, tiled=True)


def body(atom_feat, atom_pos, atom_counts, atom_nbrs, probe_pos, probe_target, tile_blocks, atom_filter, probe_filter,
         mix_weight, readout):
    blocks, channels, width = atom_feat.shape
    tiles, reads = tile_blocks.shape
    probes = probe_pos.shape[2]
    filters = atom_filter.shape[1] // channels
    peers = lax.axis_size("tile")
    spaces = lax.axis_size("space")
    devices = peers * spaces
    slots = peers * 2
    up = [(i, (i + 1) % spaces) for i in range(spaces)]
    down = [(i, (i - 1) % spaces) for i in range(spaces)]

    feat_lo = lax.ppermute(atom_feat, "space", up)
    feat_hi = lax.ppermute(atom_feat, "space", down)
    smem = pl.BlockSpec(memory_space=pltpu.SMEM)
    vmem = pl.BlockSpec(memory_space=pltpu.VMEM)
    where = jnp.transpose(atom_pos, (1, 0, 2))
    early, marked, info = pl.pallas_call(
        setup_kernel,
        in_specs=[smem, smem, vmem],
        out_specs=[vmem, vmem, smem],
        out_shape=(
            jax.ShapeDtypeStruct((peers, 3 * blocks + AUG, width), BF16),
            jax.ShapeDtypeStruct(where.shape, BF16),
            jax.ShapeDtypeStruct((3, tiles * reads), jnp.int32),
        ),
        scratch_shapes=[pltpu.SMEM((slots,), jnp.int32)],
        name="requests",
        compiler_params=pltpu.CompilerParams(vmem_limit_bytes=4 << 20),
    )(tile_blocks, atom_counts, where)
    pos_lo = lax.ppermute(marked, "space", up)
    pos_hi = lax.ppermute(marked, "space", down)
    early = lax.all_to_all(early, "tile", 0, 0, tiled=True)

    pairs = blocks * 4 * width * width

    def before(shape):
        return pl.BlockSpec((1, *shape[1:]), lambda b, *_: (jnp.maximum(b - 1, 0),) + (0,) * (len(shape) - 1))

    sums_shape = (blocks, filters * channels, width)
    sums, slope, done = call(
        functools.partial(atom_kernel, peers), (blocks + 1,), (atom_nbrs.T,),
        (feat_lo, atom_feat, feat_hi, pos_lo, marked, pos_hi, atom_filter),
        [whole(atom_feat.shape)] * 3 + [whole(marked.shape)] * 3 + [whole(atom_filter.shape)],
        (
            jax.ShapeDtypeStruct(sums_shape, BF16),
            jax.ShapeDtypeStruct(atom_feat.shape, F32),
            jax.ShapeDtypeStruct(atom_feat.shape, BF16),
        ),
        [before(sums_shape), before(atom_feat.shape), before(atom_feat.shape)],
        [
            pltpu.VMEM((3 * blocks, AUG, width), BF16),
            pltpu.VMEM((3, blocks, width), F32),
            pltpu.VMEM((blocks, AUG, width), BF16),
            pltpu.VMEM((2, 4, channels, width), BF16),
            pltpu.VMEM((2, filters, 4 * width, width), BF16),
        ],
        (2 * pairs * filters * channels, 8 << 20, 3 * pairs), 49 << 20,
    )
    asked = early[:, blocks * 3, :2].astype(jnp.int32).reshape(slots)
    sent = done.at[asked].get(mode="promise_in_bounds")
    replies = lax.all_to_all(
        sent.reshape(peers, 2 * channels, width), "tile", 0, 0, tiled=True
    ).reshape(slots, channels, width)

    pairs = tiles * reads * width * probes
    rows_shape = (tiles * reads, AUG, width)
    ready_shape = (READY, filters, probes // 128, width, 128)
    rows, goals, ready = plain(
        rows_kernel, (info, early, jnp.transpose(probe_pos, (1, 0, 2))), [SMEM, VMEM, VMEM],
        [VMEM, VMEM, pl.BlockSpec(memory_space=pl.ANY)],
        (
            jax.ShapeDtypeStruct(rows_shape, BF16),
            jax.ShapeDtypeStruct((tiles, probes // 128, AUG, 128), BF16),
            jax.ShapeDtypeStruct(ready_shape, BF16),
        ),
        [pltpu.VMEM(early.shape, F32), pltpu.VMEM(ready_shape, BF16), pltpu.SemaphoreType.DMA((READY,))],
        50 << 20, (1 << 30, 4 << 20, 1 << 20),
    )
    density, grad_probe, grad_mix, grad_read, back = plain(
        probe_kernel, (info, ready, rows, goals, replies, probe_target, probe_filter, mix_weight, readout.reshape(1, channels)),
        [SMEM, pl.BlockSpec(memory_space=pl.ANY)] + [VMEM] * 7, [VMEM] * 5,
        (
            jax.ShapeDtypeStruct((tiles, probes), F32),
            jax.ShapeDtypeStruct(probe_filter.shape, F32),
            jax.ShapeDtypeStruct(mix_weight.shape, F32),
            jax.ShapeDtypeStruct((1, channels), F32),
            jax.ShapeDtypeStruct(replies.shape, BF16),
        ),
        [pltpu.VMEM((filters, probes // 128, reads * width, 128), BF16) for _ in range(tiles)]
        + [
            pltpu.SemaphoreType.DMA((READY,)),
            pltpu.VMEM((probes // 128, filters * channels, 128), BF16),
            pltpu.VMEM((probes // 128, channels, 128), BF16),
            pltpu.VMEM((probes // 128, channels, 128), BF16),
            pltpu.VMEM((probes // 128, channels, 128), BF16),
            pltpu.VMEM((channels, 256), F32),
            pltpu.VMEM((filters * probes // 128, channels, 128), BF16),
            pltpu.VMEM(replies.shape, F32),
        ],
        50 << 20, (4 * pairs * filters * channels, 4 << 20, 3 * pairs),
    )
    returned = lax.all_to_all(
        back.reshape(peers, 2 * channels, width), "tile", 0, 0, tiled=True
    ).reshape(slots, channels, width)

    columns = 256
    part_shape = (devices, 24, width)
    parts = call(
        owner_kernel, (filters * channels // columns,), (asked,),
        (returned, slope, sums, grad_probe, grad_mix, grad_read),
        [whole(returned.shape), whole(slope.shape), pl.BlockSpec((blocks, columns, width), lambda j, *_: (0, j, 0)),
         whole(grad_probe.shape), whole(grad_mix.shape), whole((1, channels))],
        jax.ShapeDtypeStruct(part_shape, BF16), whole(part_shape),
        [pltpu.VMEM(slope.shape, F32), pltpu.VMEM(slope.shape, BF16)],
        (2 * blocks * width * channels * filters * channels, 8 << 20, 0), 49 << 20,
    )
    sums = reduced(parts)

    def filter_of(tiled):
        tall = tiled.reshape(channels // 8, filters, 8, channels)
        return jnp.transpose(tall, (0, 2, 1, 3)).reshape(channels, filters * channels).astype(F32)

    return (
        density,
        filter_of(sums[:, :8]),
        filter_of(sums[:, 8:16]),
        sums[: channels // 8, 16:].reshape(channels, channels).astype(F32),
        sums[channels // 8, 16].astype(F32),
    )


def solution(mesh):
    split2 = P(BOTH, None)
    split3d = P(BOTH, None, None)
    in_specs = (split3d, split3d, P(BOTH), split2, split3d, split2, split2, P(), P(), P(), P())
    out_specs = (split2, P(), P(), P(), P())
    return jax.shard_map(body, mesh=mesh, in_specs=in_specs, out_specs=out_specs, check_vma=False)
```

```python
import functools
import math

import jax
import jax.numpy as jnp
import numpy as np
from jax import lax
from jax.experimental import pallas as pl
from jax.experimental.pallas import tpu as pltpu
from jax.sharding import PartitionSpec as P

BOTH = ("space", "tile")
F32 = jnp.float32
BF16 = jnp.bfloat16

CUTOFF = 6.0
SPACING = 0.75
SPREAD = 0.75
SOFT = 0.01
AUG = 16
READY = (0, 1, 2, 8, 9, 10, 11, 12, 13, 14, 15)
MARK = 32.0


def envelope_terms(degree=4):
    top = CUTOFF * CUTOFF
    nodes = 0.5 * top * (1.0 - np.cos(np.pi * (np.arange(64) + 0.5) / 64))
    values = np.cos(np.pi * np.sqrt(nodes) / (2 * CUTOFF)) / (top - nodes)
    fit = np.polynomial.chebyshev.Chebyshev.fit(nodes, values, degree, domain=[0.0, top])
    return [float(c) for c in fit.convert(kind=np.polynomial.Polynomial).coef]


ENVELOPE = envelope_terms()


def radial_store(square, factor, filters, store):
    distance = square * lax.rsqrt(square)
    root = math.sqrt(factor)
    poly = jnp.full_like(square, ENVELOPE[-1] * root)
    for term in ENVELOPE[-2::-1]:
        poly = poly * square + term * root
    half = jnp.maximum(CUTOFF * CUTOFF - square, 0.0) * poly
    value = (half * half) * jnp.exp2(square * (-math.log2(math.e) / SPREAD**2))
    growth = jnp.exp2(distance * (2.0 * math.log2(math.e) * SPACING / SPREAD**2))
    for r in range(filters):
        store(r, value.astype(BF16))
        if r + 1 < filters:
            value = value * growth


def decay(r):
    return math.exp(-((r * SPACING / SPREAD) ** 2))


def sigmoid(values):
    return 1.0 / (1.0 + jnp.exp(-values))


def dot(a, b, contract):
    return lax.dot_general(a, b, ((contract[0:1], contract[1:2]), ((), ())), preferred_element_type=F32)


def stacked(rows):
    at = lax.broadcasted_iota(jnp.int32, (AUG, rows[0].shape[1]), 0)
    out = jnp.zeros(at.shape, F32)
    for i, row in enumerate(rows):
        out = jnp.where(at == i, row, out)
    return out.astype(BF16)


def pieces(values):
    high = values.astype(BF16).astype(F32)
    rest = values - high
    middle = rest.astype(BF16).astype(F32)
    return [high, middle, rest - middle]


def source_rows(x, y, z):
    unit = jnp.ones_like(x)
    return stacked([x, y, z] * 3 + pieces(x * x + y * y + z * z) + [unit] * 3)


def target_rows(x, y, z):
    unit = jnp.ones_like(x)
    parts = [pieces(-2.0 * row) for row in (x, y, z)]
    rows = [part[i] for i in range(3) for part in parts]
    return stacked(rows + [unit] * 3 + pieces(x * x + y * y + z * z + SOFT))


def setup_kernel(reads_ref, counts_ref, where_ref, early_ref, marked_ref, info_ref, asks):
    peers = early_ref.shape[0]
    blocks = where_ref.shape[1]
    width = where_ref.shape[2]
    tiles, reads = reads_ref.shape
    owners, spots = [], []
    for t in range(tiles):
        for k in range(reads):
            block = reads_ref[t, k]
            owners.append(lax.rem(lax.div(block, blocks), peers))
            spots.append(lax.rem(block, blocks))
    for i in range(2 * peers):
        asks[i] = 0
    for i, (owner, spot) in enumerate(zip(owners, spots)):
        rank = jnp.int32(0)
        for j in range(len(owners)):
            if j != i:
                rank = jnp.where((owners[j] == owner) & (spots[j] < spot), 1, rank)
        slot = owner * 2 + rank
        info_ref[0, i] = slot
        info_ref[1, i] = owner
        info_ref[2, i] = spot
        asks[slot] = spot
    line = lax.broadcasted_iota(jnp.int32, (blocks, width), 0)
    lane = lax.broadcasted_iota(jnp.int32, (blocks, width), 1)
    counts = jnp.zeros((blocks, width), jnp.int32)
    for i in range(blocks):
        counts = jnp.where(line == i, counts_ref[i], counts)
    for c in range(3):
        marked_ref[c] = jnp.where(lane < counts, where_ref[c].astype(F32), 2.0 * MARK).astype(BF16)
    lane = lax.broadcasted_iota(jnp.int32, (AUG, width), 1)
    for t in range(peers):
        for c in range(3):
            early_ref[t, c * blocks : (c + 1) * blocks, :] = where_ref[c]
        note = jnp.where(lane == 0, asks[2 * t], jnp.where(lane == 1, asks[2 * t + 1], 0))
        early_ref[t, 3 * blocks :, :] = note.astype(F32).astype(BF16)


def atom_kernel(peers, nbr_ref, lo_ref, own_hbm, hi_ref, lo_pos, own_pos, hi_pos, weight_hbm,
                sums_ref, slope_ref, done_ref, own_ref, weight_ref, landed, rows, masks, goals, feat, kern, both):
    b = pl.program_id(0)
    blocks, channels, width = own_ref.shape
    nbrs = feat.shape[1]
    filters = kern.shape[1]
    scale = (nbrs * width) ** -0.5

    @pl.when(b == 0)
    def _():
        fetches = [
            pltpu.make_async_copy(own_hbm, own_ref, landed.at[0]),
            pltpu.make_async_copy(weight_hbm, weight_ref, landed.at[1]),
        ]
        for copy in fetches:
            copy.start()
        for s, pos in enumerate((lo_pos, own_pos, hi_pos)):
            wide = [pos[c].astype(F32) for c in range(3)]
            there = wide[0] < MARK
            wide = [jnp.where(there, w, 0.0) for w in wide]
            masks[s] = there.astype(F32)
            for i in range(blocks):
                x, y, z = (w[i : i + 1, :] for w in wide)
                rows[s * blocks + i] = source_rows(x, y, z)
                if s == 1:
                    goals[i] = target_rows(x, y, z)
        for copy in fetches:
            copy.wait()

    def pick(slot, k, feats, s, index):
        mask = jnp.broadcast_to(masks[s, pl.ds(index, 1), :], (channels, width)).astype(BF16)
        feat[slot, k] = feats[index] * mask

    def prepare(slot, k, index):
        square = dot(rows[index], goals[jnp.minimum(b, blocks - 1)], (0, 0))

        def store(r, value):
            kern[slot, r, k * width : (k + 1) * width, :] = value

        radial_store(square, scale, filters, store)

    def finish(slot, r):
        feats = jnp.concatenate([feat[slot, k] for k in range(nbrs)], axis=1)
        kerns = jnp.concatenate([kern[slot, r], kern[slot, r + 1]], axis=1)
        part = dot(feats, kerns, (1, 0))
        for i in range(2):
            piece = part[:, i * width : (i + 1) * width] * decay(r + i)
            piece = piece.astype(BF16)
            lines = slice((r + i) * channels, (r + i + 1) * channels)
            sums_ref[0, lines, :] = piece
            both[slot, lines, :] = piece

    def last(slot, at):
        sums = both[slot]
        message = dot(weight_ref[...], sums, (1, 0))
        mask = masks[1, pl.ds(at, 1), :]
        gate = sigmoid(message)
        slope_ref[0] = gate * (1.0 + message * (1.0 - gate)) * mask
        done_ref[0] = ((own_ref[at].astype(F32) + message * gate) * mask).astype(BF16)

    def step(slot):
        at = jnp.minimum(b, blocks - 1)
        picked = [nbr_ref[k, at] for k in range(nbrs)]
        index = [lax.rem(block, blocks) for block in picked]
        space = [lax.div(block, blocks * peers) for block in picked]
        side = jnp.where(space[3] == space[2], 1, jnp.where(space[3] == space[0], 0, 2))
        sides = [0, 2, 1, side]
        pick(slot, 0, lo_ref, 0, index[0])
        pick(slot, 1, hi_ref, 2, index[1])
        pick(slot, 2, own_ref, 1, index[2])
        for s, feats in enumerate((lo_ref, own_ref, hi_ref)):
            @pl.when(side == s)
            def _():
                pick(slot, 3, feats, s, index[3])

        for k in range(nbrs):
            prepare(slot, k, sides[k] * blocks + index[k])
            finish(1 - slot, 2 * k)
            if k == 1:
                last(slot, jnp.clip(b - 2, 0, blocks - 1))

    @pl.when(b % 2 == 0)
    def _():
        step(0)

    @pl.when(b % 2 == 1)
    def _():
        step(1)


def radial_block(rows, goals_ref, t, scale, filters, store):
    for at in range(goals_ref.shape[1]):
        square = dot(rows, goals_ref[t, at], (0, 0))
        radial_store(square, scale, filters, functools.partial(store, at))


def rows_kernel(info_ref, early_ref, probe_ref, rows_ref, goals_ref, kern_ref, places, held, left):
    blocks = (early_ref.shape[1] - AUG) // 3
    width = early_ref.shape[2]
    reads = rows_ref.shape[0] // goals_ref.shape[0]
    scale = (reads * width) ** -0.5
    places[...] = early_ref[...].astype(F32)
    for b in range(rows_ref.shape[0]):
        owner, spot = info_ref[1, b], info_ref[2, b]
        rows_ref[b] = source_rows(*(places[owner, pl.ds(c * blocks + spot, 1), :] for c in range(3)))
    for t in range(goals_ref.shape[0]):
        goal = target_rows(*(probe_ref[c, t : t + 1, :] for c in range(3)))
        for at in range(goals_ref.shape[1]):
            goals_ref[t, at] = goal[:, at * 128 : (at + 1) * 128]

    def leave(k):
        return pltpu.make_async_copy(held.at[k], kern_ref.at[k], left.at[k])

    for k, block in enumerate(READY):
        def store(at, r, value):
            held[k, r, at] = value

        radial_block(rows_ref[block], goals_ref, block // reads, scale, held.shape[1], store)
        leave(k).start()
    for k in range(held.shape[0]):
        leave(k).wait()


def probe_kernel(info_ref, ready_ref, rows_ref, goals_ref, reply_ref, goal_ref, weight_ref, mix_ref, read_ref,
                 density_ref, probe_ref, mixg_ref, readg_ref, back_ref,
                 first, second, arrived, sums, squashed, grads_mixed, grads_hidden, slopes, grads, total):
    _, channels, width = reply_ref.shape
    tiles, probes = goal_ref.shape
    filters, chunks = first.shape[:2]
    reads = rows_ref.shape[0] // tiles
    ready = ready_ref.shape[0]
    scale = (reads * width) ** -0.5
    kerns = (first, second)

    def fetch(k):
        t, at = divmod(READY[k], reads)
        return pltpu.make_async_copy(
            ready_ref.at[k], kerns[t].at[:, :, at * width : (at + 1) * width, :], arrived.at[k]
        )

    for k in range(ready):
        fetch(k).start()
    line = lax.broadcasted_iota(jnp.int32, (channels, channels), 0)
    diagonal = line == lax.broadcasted_iota(jnp.int32, (channels, channels), 1)
    readout = jnp.sum(jnp.where(diagonal, read_ref[...], 0.0), axis=1, keepdims=True)
    total[...] = jnp.zeros_like(total)

    def radial(t, k):
        def store(at, r, value):
            kerns[t][r, at, pl.ds(pl.multiple_of(k * width, width), width), :] = value

        radial_block(rows_ref[t * reads + k], goals_ref, t, scale, filters, store)

    def forward(t):
        feats = jnp.concatenate([reply_ref[info_ref[0, t * reads + k]] for k in range(reads)], axis=1)
        for r in range(filters):
            for at in range(0, chunks, 2):
                right = jnp.concatenate([kerns[t][r, at], kerns[t][r, at + 1]], axis=1)
                part = (dot(feats, right, (1, 0)) * decay(r)).astype(BF16)
                for i in range(2):
                    sums[at + i, r * channels : (r + 1) * channels, :] = part[:, i * 128 : (i + 1) * 128]

    def halves(ref, at, value):
        for i in range(2):
            ref[at + i] = value[:, i * 128 : (i + 1) * 128]

    def middle(t):
        grad_read = jnp.zeros((channels, 1), F32)
        for at in range(0, chunks, 2):
            span = slice(at * 128, (at + 2) * 128)
            hidden = dot(weight_ref[...], jnp.concatenate([sums[at], sums[at + 1]], axis=1), (1, 0))
            gate = sigmoid(hidden)
            squash = (hidden * gate).astype(BF16)
            halves(squashed, at, squash)
            slopes[...] = gate * (1.0 + hidden * (1.0 - gate))
            mixed = dot(mix_ref[...], squash, (1, 0))
            outer_gate = sigmoid(mixed)
            outer = mixed * outer_gate
            density = jnp.sum(readout * outer, axis=0, keepdims=True)
            density_ref[t : t + 1, span] = density
            misfit = (density - goal_ref[t : t + 1, span]) * (1.0 / probes)
            grad_read = grad_read + jnp.sum(outer * misfit, axis=1, keepdims=True)
            grad_mixed = (readout * misfit * (outer_gate * (1.0 + mixed * (1.0 - outer_gate)))).astype(BF16)
            halves(grads_mixed, at, grad_mixed)
            halves(grads_hidden, at, (dot(mix_ref[...], grad_mixed, (0, 0)) * slopes[...]).astype(BF16))
        grad_read = jnp.sum(jnp.where(diagonal, grad_read, 0.0), axis=0, keepdims=True)

        def joined(ref):
            return jnp.concatenate([ref[at] for at in range(chunks)], axis=1)

        grad_hidden = joined(grads_hidden)
        grad_mix = dot(joined(grads_mixed), joined(squashed), (1, 1))
        grad_probe = dot(grad_hidden, joined(sums), (1, 1))
        if t == 0:
            readg_ref[...], mixg_ref[...], probe_ref[...] = grad_read, grad_mix, grad_probe
        else:
            readg_ref[...] += grad_read
            mixg_ref[...] += grad_mix
            probe_ref[...] += grad_probe
        for r in range(filters):
            part = dot(weight_ref[:, r * channels : (r + 1) * channels], grad_hidden, (0, 0)) * decay(r)
            part = part.astype(BF16)
            for at in range(chunks):
                grads[r * chunks + at] = part[:, at * 128 : (at + 1) * 128]

    def backward(t):
        all_grads = jnp.concatenate([grads[i] for i in range(filters * chunks)], axis=1)
        for k in range(0, reads, 2):
            lines = slice(k * width, (k + 2) * width)
            right = jnp.concatenate(
                [kerns[t][r, at, lines, :] for r in range(filters) for at in range(chunks)], axis=1
            )
            part = dot(all_grads, right, (1, 1))
            for i in range(2):
                slot = info_ref[0, t * reads + k + i]
                total[slot] += part[:, i * width : (i + 1) * width]

    for t in reversed(range(tiles)):
        @pl.loop(sum(block // reads == t for block in READY), reads)
        def _(k):
            radial(t, k)

    for t in range(tiles):
        for k, block in enumerate(READY):
            if block // reads == t:
                fetch(k).wait()
        forward(t)
        middle(t)
        backward(t)
    back_ref[...] = total[...].astype(BF16)


def owner_kernel(asked_ref, back_ref, slope_ref, sums_ref, probe_ref, mix_ref, read_ref, out_ref, total, grads):
    step = pl.program_id(0)
    blocks, channels, width = slope_ref.shape
    columns = sums_ref.shape[1]
    across = probe_ref.shape[1] // width
    high = 8

    @pl.when(step == 0)
    def _():
        total[...] = jnp.zeros_like(total)

        def gather(i, carry):
            at = asked_ref[i]
            total[at] = total[at] + back_ref[i].astype(F32)
            return carry

        lax.fori_loop(0, back_ref.shape[0], gather, 0)
        for b in range(blocks):
            grads[b] = (total[b] * slope_ref[b]).astype(BF16)
        for i in range(channels // high):
            lines = slice(i * high, (i + 1) * high)
            for j in range(across):
                out_ref[i * across + j, high : 2 * high, :] = probe_ref[lines, j * width : (j + 1) * width].astype(BF16)
            out_ref[i, 2 * high :, :] = mix_ref[lines, :].astype(BF16)
        out_ref[channels // high, 2 * high :, :] = jnp.broadcast_to(read_ref[...], (high, width)).astype(BF16)
        for i in range(channels // high + 1, out_ref.shape[0]):
            out_ref[i, 2 * high :, :] = jnp.zeros((high, width), BF16)

    all_grads = jnp.concatenate([grads[b] for b in range(blocks)], axis=1)
    all_sums = jnp.concatenate([sums_ref[b] for b in range(blocks)], axis=1)
    part = dot(all_grads, all_sums, (1, 1)).astype(BF16)
    for i in range(channels // high):
        for j in range(columns // width):
            out_ref[i * across + step * (columns // width) + j, :high, :] = part[
                i * high : (i + 1) * high, j * width : (j + 1) * width
            ]


def spread_kernel(parts_ref, out_ref):
    mine = jnp.sum(parts_ref[...].astype(F32), axis=0, keepdims=True).astype(BF16)
    out_ref[...] = jnp.broadcast_to(mine, out_ref.shape)


def whole(shape):
    return pl.BlockSpec(shape, lambda *_: (0,) * len(shape))


def call(kernel, grid, prefetch, ins, in_specs, outs, out_specs, scratch, cost, limit=None):
    return pl.pallas_call(
        kernel,
        grid_spec=pltpu.PrefetchScalarGridSpec(
            num_scalar_prefetch=len(prefetch), grid=grid, in_specs=in_specs, out_specs=out_specs,
            scratch_shapes=scratch,
        ),
        out_shape=outs,
        cost_estimate=pl.CostEstimate(flops=cost[0], bytes_accessed=cost[1], transcendentals=cost[2]),
        compiler_params=pltpu.CompilerParams(vmem_limit_bytes=limit),
    )(*prefetch, *ins)


SMEM = pl.BlockSpec(memory_space=pltpu.SMEM)
VMEM = pl.BlockSpec(memory_space=pltpu.VMEM)
HBM = pl.BlockSpec(memory_space=pltpu.HBM)


def in_hbm(value):
    return pltpu.with_memory_space_constraint(value, pltpu.HBM)


def plain(kernel, ins, in_specs, out_specs, outs, scratch, limit, cost=None):
    return pl.pallas_call(
        kernel, in_specs=in_specs, out_specs=out_specs, out_shape=outs, scratch_shapes=scratch,
        cost_estimate=cost and pl.CostEstimate(flops=cost[0], bytes_accessed=cost[1], transcendentals=cost[2]),
        compiler_params=pltpu.CompilerParams(vmem_limit_bytes=limit),
    )(*ins)


def reduced(chunks):
    sent = lax.all_to_all(chunks, BOTH, 0, 0, tiled=True)
    vmem = pl.BlockSpec(memory_space=pltpu.VMEM)
    totals = pl.pallas_call(
        spread_kernel, in_specs=[vmem], out_specs=vmem, out_shape=jax.ShapeDtypeStruct(sent.shape, BF16), name="spread",
        compiler_params=pltpu.CompilerParams(vmem_limit_bytes=4 << 20),
    )(sent)
    return lax.all_to_all(totals, BOTH, 0, 0, tiled=True)


def body(atom_feat, atom_pos, atom_counts, atom_nbrs, probe_pos, probe_target, tile_blocks, atom_filter, probe_filter,
         mix_weight, readout):
    blocks, channels, width = atom_feat.shape
    tiles, reads = tile_blocks.shape
    probes = probe_pos.shape[2]
    filters = atom_filter.shape[1] // channels
    peers = lax.axis_size("tile")
    spaces = lax.axis_size("space")
    devices = peers * spaces
    slots = peers * 2
    up = [(i, (i + 1) % spaces) for i in range(spaces)]
    down = [(i, (i - 1) % spaces) for i in range(spaces)]

    feat_lo = lax.ppermute(atom_feat, "space", up)
    feat_hi = lax.ppermute(atom_feat, "space", down)
    smem = pl.BlockSpec(memory_space=pltpu.SMEM)
    vmem = pl.BlockSpec(memory_space=pltpu.VMEM)
    where = jnp.transpose(atom_pos, (1, 0, 2))
    early, marked, info = pl.pallas_call(
        setup_kernel,
        in_specs=[smem, smem, vmem],
        out_specs=[vmem, vmem, smem],
        out_shape=(
            jax.ShapeDtypeStruct((peers, 3 * blocks + AUG, width), BF16),
            jax.ShapeDtypeStruct(where.shape, BF16),
            jax.ShapeDtypeStruct((3, tiles * reads), jnp.int32),
        ),
        scratch_shapes=[pltpu.SMEM((slots,), jnp.int32)],
        name="requests",
        compiler_params=pltpu.CompilerParams(vmem_limit_bytes=4 << 20),
    )(in_hbm(tile_blocks), in_hbm(atom_counts), in_hbm(where))
    pos_lo = lax.ppermute(marked, "space", up)
    pos_hi = lax.ppermute(marked, "space", down)
    early = lax.all_to_all(early, "tile", 0, 0, tiled=True)

    pairs = blocks * 4 * width * width

    def before(shape, steps):
        def index(b, *_):
            return (jnp.clip(b - steps, 0, blocks - 1),) + (0,) * (len(shape) - 1)

        return pl.BlockSpec((1, *shape[1:]), index)

    sums_shape = (blocks, filters * channels, width)
    sums, slope, done = call(
        functools.partial(atom_kernel, peers), (blocks + 2,), (in_hbm(atom_nbrs.T),),
        (feat_lo, in_hbm(atom_feat), feat_hi, pos_lo, marked, pos_hi, in_hbm(atom_filter)),
        [whole(atom_feat.shape), HBM, whole(atom_feat.shape)] + [whole(marked.shape)] * 3 + [HBM],
        (
            jax.ShapeDtypeStruct(sums_shape, BF16),
            jax.ShapeDtypeStruct(atom_feat.shape, F32),
            jax.ShapeDtypeStruct(atom_feat.shape, BF16),
        ),
        [before(sums_shape, 1), before(atom_feat.shape, 2), before(atom_feat.shape, 2)],
        [
            pltpu.VMEM(atom_feat.shape, BF16),
            pltpu.VMEM(atom_filter.shape, BF16),
            pltpu.SemaphoreType.DMA((2,)),
            pltpu.VMEM((3 * blocks, AUG, width), BF16),
            pltpu.VMEM((3, blocks, width), F32),
            pltpu.VMEM((blocks, AUG, width), BF16),
            pltpu.VMEM((2, 4, channels, width), BF16),
            pltpu.VMEM((2, filters, 4 * width, width), BF16),
            pltpu.VMEM((2, filters * channels, width), BF16),
        ],
        (2 * pairs * filters * channels, 8 << 20, 3 * pairs), 49 << 20,
    )
    asked = early[:, blocks * 3, :2].astype(jnp.int32).reshape(slots)
    sent = done.at[asked].get(mode="promise_in_bounds")
    replies = lax.all_to_all(
        sent.reshape(peers, 2 * channels, width), "tile", 0, 0, tiled=True
    ).reshape(slots, channels, width)

    pairs = tiles * reads * width * probes
    rows_shape = (tiles * reads, AUG, width)
    ready_shape = (len(READY), filters, probes // 128, width, 128)
    rows, goals, ready = plain(
        rows_kernel, (info, early, jnp.transpose(probe_pos, (1, 0, 2))), [SMEM, VMEM, VMEM],
        [VMEM, VMEM, pl.BlockSpec(memory_space=pl.ANY)],
        (
            jax.ShapeDtypeStruct(rows_shape, BF16),
            jax.ShapeDtypeStruct((tiles, probes // 128, AUG, 128), BF16),
            jax.ShapeDtypeStruct(ready_shape, BF16),
        ),
        [pltpu.VMEM(early.shape, F32), pltpu.VMEM(ready_shape, BF16), pltpu.SemaphoreType.DMA((len(READY),))],
        50 << 20, (1 << 30, 4 << 20, 1 << 20),
    )
    density, grad_probe, grad_mix, grad_read, back = plain(
        probe_kernel, (info, ready, rows, goals, replies, probe_target, probe_filter, mix_weight, readout.reshape(1, channels)),
        [SMEM, pl.BlockSpec(memory_space=pl.ANY)] + [VMEM] * 7, [VMEM] * 5,
        (
            jax.ShapeDtypeStruct((tiles, probes), F32),
            jax.ShapeDtypeStruct(probe_filter.shape, F32),
            jax.ShapeDtypeStruct(mix_weight.shape, F32),
            jax.ShapeDtypeStruct((1, channels), F32),
            jax.ShapeDtypeStruct(replies.shape, BF16),
        ),
        [pltpu.VMEM((filters, probes // 128, reads * width, 128), BF16) for _ in range(tiles)]
        + [
            pltpu.SemaphoreType.DMA((len(READY),)),
            pltpu.VMEM((probes // 128, filters * channels, 128), BF16),
            pltpu.VMEM((probes // 128, channels, 128), BF16),
            pltpu.VMEM((probes // 128, channels, 128), BF16),
            pltpu.VMEM((probes // 128, channels, 128), BF16),
            pltpu.VMEM((channels, 256), F32),
            pltpu.VMEM((filters * probes // 128, channels, 128), BF16),
            pltpu.VMEM(replies.shape, F32),
        ],
        50 << 20, (4 * pairs * filters * channels, 4 << 20, 3 * pairs),
    )
    returned = lax.all_to_all(
        back.reshape(peers, 2 * channels, width), "tile", 0, 0, tiled=True
    ).reshape(slots, channels, width)

    columns = 256
    part_shape = (devices, 24, width)
    parts = call(
        owner_kernel, (filters * channels // columns,), (asked,),
        (returned, slope, sums, grad_probe, grad_mix, grad_read),
        [whole(returned.shape), whole(slope.shape), pl.BlockSpec((blocks, columns, width), lambda j, *_: (0, j, 0)),
         whole(grad_probe.shape), whole(grad_mix.shape), whole((1, channels))],
        jax.ShapeDtypeStruct(part_shape, BF16), whole(part_shape),
        [pltpu.VMEM(slope.shape, F32), pltpu.VMEM(slope.shape, BF16)],
        (2 * blocks * width * channels * filters * channels, 8 << 20, 0), 49 << 20,
    )
    sums = reduced(parts)

    def filter_of(tiled):
        tall = tiled.reshape(channels // 8, filters, 8, channels)
        return jnp.transpose(tall, (0, 2, 1, 3)).reshape(channels, filters * channels).astype(F32)

    return (
        density,
        filter_of(sums[:, :8]),
        filter_of(sums[:, 8:16]),
        sums[: channels // 8, 16:].reshape(channels, channels).astype(F32),
        sums[channels // 8, 16].astype(F32),
    )


def solution(mesh):
    split2 = P(BOTH, None)
    split3d = P(BOTH, None, None)
    in_specs = (split3d, split3d, P(BOTH), split2, split3d, split2, split2, P(), P(), P(), P())
    out_specs = (split2, P(), P(), P(), P())
    return jax.shard_map(body, mesh=mesh, in_specs=in_specs, out_specs=out_specs, check_vma=False)
```
